32 devices in a mesh: dp: 4 (over y, core), row: 2 (over x), col: 4 (over z).
Axes of the slice: x: 2, y: 2, z: 4, core: 2. Of those that a mesh axis runs over, the one named last changes fastest.
Arguments:
- block_in: bfloat16 [2048, 1024], P(('dp', 'row'), 'col'), may hold values from -6 to 6
- cotangent: bfloat16 [2048, 1024], P(('dp', 'row'), 'col'), may hold values from -6 to 6
- segments: int32 [2048], P('dp'), may hold values from 0 to 18, as said below
- positions: int32 [2048], P('dp'), may hold values from 0 to 511, as said below
- attn_gain: float32 [1024], P('col'), may hold values from 0.5 to 1.5
- attn_shift: float32 [1024], P('col'), may hold values from -1.5 to 1.5
- mlp_gain: float32 [1024], P('col'), may hold values from 0.5 to 1.5
- mlp_shift: float32 [1024], P('col'), may hold values from -1.5 to 1.5
- qkv_weight: bfloat16 [1024, 3072], P('col', 'row'), may hold values from -0.1875 to 0.1875
- qkv_bias: float32 [3072], P(('row', 'col')), may hold values from -2.5 to 2.5
- out_weight: bfloat16 [1024, 1024], P('row', 'col'), may hold values from -1.5 to 1.5
- out_bias: float32 [1024], P('col'), may hold values from -2.5 to 2.5
- up_weight: bfloat16 [1024, 4096], P('col', 'row'), may hold values from -0.1875 to 0.1875
- up_bias: float32 [4096], P(('row', 'col')), may hold values from -2.5 to 2.5
- down_weight: bfloat16 [4096, 1024], P('row', 'col'), may hold values from -0.09375 to 0.09375
- down_bias: float32 [1024], P('col'), may hold values from -2.5 to 2.5
Outputs:
- block_out: bfloat16 [2048, 1024], P(('dp', 'row'), 'col')
- grad_in: bfloat16 [2048, 1024], P(('dp', 'row'), 'col')
- grad_qkv_weight: float32 [1024, 3072], P('col', 'row')
- grad_qkv_bias: float32 [3072], P(('row', 'col'))
- grad_out_weight: float32 [1024, 1024], P('row', 'col')
- grad_out_bias: float32 [1024], P('col')
- grad_up_weight: float32 [1024, 4096], P('col', 'row')
- grad_up_bias: float32 [4096], P(('row', 'col'))
- grad_down_weight: float32 [4096, 1024], P('row', 'col')
- grad_down_bias: float32 [1024], P('col')
- grad_attn_gain: float32 [1024], P('col')
- grad_attn_shift: float32 [1024], P('col')
- grad_mlp_gain: float32 [1024], P('col')
- grad_mlp_shift: float32 [1024], P('col')
The draws below stay inside these ranges and needn't reach their ends.
Inputs may be any that keep to these rules, and one draw needn't show every extreme that they name: segments never fall along the tokens, and every packed sequence of 512 tokens begins a new segment. `positions`: a token's position is the number of tokens before it in its segment.
All inputs are finite; a program needn't handle non-finite values.
Results may differ from the reference program's by a relative error of at most 0.011.
Values may be sent and summed in bfloat16 or wider, within the bound.
No kernel may reach another device: no remote copies, remote signals or barrier semaphores. Data moves between devices by JAX's collectives and lax.ppermute only.
A program may use at most 64 MiB of HBM per device.

```python
import math
import jax
import jax.numpy as jnp
from jax import lax

D = 1024
HEADS = 16
HD = 64
FF = 4096
PACK = 512
ROT = 16
TOKENS = 2048
N_DP = 4


extra_starts = 5


def layout_flags(key):
    total_tokens = PACK * N_DP
    index = jnp.arange(total_tokens, dtype=jnp.int32)
    pack_keys = jax.random.split(jax.random.fold_in(key, 11), N_DP)
    orders = jax.vmap(lambda one_key: jax.random.permutation(one_key, PACK - 1))(pack_keys)
    chosen = orders[:, :extra_starts].astype(jnp.int32) + 1
    inner = jnp.arange(PACK, dtype=jnp.int32)
    marked = jnp.any(inner[None, None, :] == chosen[:, :, None], axis=1)
    first_pack = (jnp.arange(N_DP, dtype=jnp.int32) == 0)[:, None]
    begins = (inner == 0)[None, :]
    flag = jnp.where(first_pack, begins, begins | marked).reshape(total_tokens)
    return (index, flag)


def draw_segments(key, part):
    index, flag = layout_flags(key)
    return (jnp.cumsum(flag.astype(jnp.int32)) - 1).astype(jnp.int32)


def draw_positions(key, part):
    index, flag = layout_flags(key)
    begin = lax.cummax(jnp.where(flag, index, 0), axis=0)
    return (index - begin).astype(jnp.int32)


def draw_qkv_bias(key, part):
    base = jnp.clip(jax.random.normal(jax.random.fold_in(key, 3), (HEADS, 3, HD), jnp.float32) * 0.5, -2.5, 2.5)
    return base.reshape(3 * D).astype(jnp.float32)


def block_levels(own_key, shape, shards, low, largest):
    level = 1.0
    for axis_at, shards_of in shards:
        heights = jax.random.uniform(jax.random.fold_in(jax.random.fold_in(own_key, 6), axis_at), (shards_of,), jnp.float32, low / len(shards), largest / len(shards))
        level = level * jnp.repeat(jnp.exp(heights), shape[axis_at] // shards_of).reshape((-1,) + (1,) * (len(shape) - 1 - axis_at))
    return level


def bell_draw(own_key, dims, scale, limit, shards=(), kind=jnp.bfloat16):
    array = scale * jax.random.normal(own_key, dims, jnp.float32)
    if shards:
        array = array * block_levels(own_key, dims, shards, -0.22, 0.18)
    return jnp.clip(array, -limit, limit).astype(kind)


def setup_inputs(seed: int = 0) -> dict:
    streams_of = jax.random.split(jax.random.key(seed), 17)
    block_in = bell_draw(streams_of[0], (TOKENS, D), 1.0, 6.0, ((0, 8), (1, 4)))
    cotangent = bell_draw(streams_of[1], (TOKENS, D), 1.0, 6.0, ((0, 8), (1, 4)))
    segments = draw_segments(jax.random.fold_in(streams_of[16], 71), 0)
    positions = draw_positions(jax.random.fold_in(streams_of[16], 71), 0)
    attn_gain = jnp.clip(1.0 + 0.1 * jax.random.normal(streams_of[4], (D,), jnp.float32), 0.5, 1.5)
    attn_shift = bell_draw(streams_of[5], (D,), 0.3, 1.5, ((0, 4),), jnp.float32)
    mlp_gain = jnp.clip(1.0 + 0.1 * jax.random.normal(streams_of[6], (D,), jnp.float32), 0.5, 1.5)
    mlp_shift = bell_draw(streams_of[7], (D,), 0.3, 1.5, ((0, 4),), jnp.float32)
    qkv_weight = bell_draw(streams_of[8], (D, 3 * D), D ** -0.5, 0.1875, ((0, 4), (1, 2)))
    qkv_bias = draw_qkv_bias(jax.random.fold_in(streams_of[16], 71), 0)
    out_weight = bell_draw(streams_of[10], (D, D), (D // 64) ** -0.5, 1.5, ((0, 2), (1, 4)))
    out_bias = bell_draw(streams_of[11], (D,), 0.5, 2.5, ((0, 4),), jnp.float32)
    up_weight = bell_draw(streams_of[12], (D, FF), D ** -0.5, 0.1875, ((0, 4), (1, 2)))
    up_bias = bell_draw(streams_of[13], (FF,), 0.5, 2.5, ((0, 8),), jnp.float32)
    down_weight = bell_draw(streams_of[14], (FF, D), FF ** -0.5, 0.09375, ((0, 2), (1, 4)))
    down_bias = bell_draw(streams_of[15], (D,), 0.5, 2.5, ((0, 4),), jnp.float32)
    return dict(block_in=block_in, cotangent=cotangent, segments=segments, positions=positions, attn_gain=attn_gain, attn_shift=attn_shift, mlp_gain=mlp_gain, mlp_shift=mlp_shift, qkv_weight=qkv_weight, qkv_bias=qkv_bias, out_weight=out_weight, out_bias=out_bias, up_weight=up_weight, up_bias=up_bias, down_weight=down_weight, down_bias=down_bias)


EPS = 1e-05
NEG = -1e+30

def rotary_tables(positions, rot_dims):
    half_dims = rot_dims // 2
    exponent = jnp.arange(half_dims, dtype=jnp.float32) * (2.0 / rot_dims)
    inverse = jnp.power(10000.0, -exponent)
    angles = positions.astype(jnp.float32)[:, None] * inverse[None, :]
    cosine = jnp.cos(angles)
    sine_tab = jnp.sin(angles)
    return (jnp.concatenate([cosine, cosine], 1), jnp.concatenate([sine_tab, sine_tab], 1))

def rotate_fwd(values, cosine, sine_tab):
    rot_dims = cosine.shape[1]
    half_dims = rot_dims // 2
    front = values[..., :rot_dims]
    turned = jnp.concatenate([-front[..., half_dims:], front[..., :half_dims]], -1)
    moved = front * cosine[:, None, :] + turned * sine_tab[:, None, :]
    return jnp.concatenate([moved, values[..., rot_dims:]], -1)

def rotate_back(grads, cosine, sine_tab):
    rot_dims = cosine.shape[1]
    half_dims = rot_dims // 2
    front = grads[..., :rot_dims]
    scaled = front * sine_tab[:, None, :]
    turned = jnp.concatenate([scaled[..., half_dims:], -scaled[..., :half_dims]], -1)
    moved = front * cosine[:, None, :] + turned
    return jnp.concatenate([moved, grads[..., rot_dims:]], -1)

def score_block(queries, keys_b, segments, start, width):
    length = keys_b.shape[0]
    raw = jnp.einsum('qhd,khd->hqk', queries.astype(jnp.float32), keys_b.astype(jnp.float32)) * (1.0 / math.sqrt(HD))
    query_pos = start + jnp.arange(width, dtype=jnp.int32)
    key_pos = jnp.arange(length, dtype=jnp.int32)
    query_seg = lax.dynamic_slice_in_dim(segments, start, width, 0)
    allowed = (key_pos[None, :] <= query_pos[:, None]) & (segments[None, :] == query_seg[:, None])
    return (jnp.where(allowed[None], raw, NEG), allowed)

def attend(queries, keys_b, values, segments):
    length, heads_here, head_dim = queries.shape
    width = min(512, length)
    count = length // width

    def one_block(index):
        start = (index * width).astype(jnp.int32)
        part = lax.dynamic_slice_in_dim(queries, start, width, 0)
        scores, allowed = score_block(part, keys_b, segments, start, width)
        top = lax.optimization_barrier(jnp.max(scores, -1, keepdims=True))
        expo = jnp.exp(scores - top)
        total = lax.optimization_barrier(jnp.sum(expo, -1, keepdims=True))
        weights = (expo / total).astype(jnp.bfloat16)
        attended = jnp.einsum('hqk,khd->qhd', weights.astype(jnp.float32), values.astype(jnp.float32))
        return (attended, (top + jnp.log(total))[..., 0])
    attended, log_total = lax.map(one_block, jnp.arange(count, dtype=jnp.int32))
    attended = attended.reshape(length, heads_here, head_dim)
    log_total = jnp.transpose(log_total, (1, 0, 2)).reshape(heads_here, length)
    return (attended, log_total)

def attend_back(queries, keys_b, values, grad_att, log_total, segments):
    length, heads_here, head_dim = queries.shape
    width = min(512, length)
    count = length // width
    scale = 1.0 / math.sqrt(HD)

    def one_block(carry, index):
        grad_keys, grad_values = carry
        start = (index * width).astype(jnp.int32)
        part_q = lax.dynamic_slice_in_dim(queries, start, width, 0)
        part_g = lax.dynamic_slice_in_dim(grad_att, start, width, 0)
        part_lse = lax.dynamic_slice_in_dim(log_total, start, width, 1)
        scores, allowed = score_block(part_q, keys_b, segments, start, width)
        probs = jnp.where(allowed[None], jnp.exp(scores - part_lse[..., None]), 0.0)
        probs_b = probs.astype(jnp.bfloat16)
        grad_values = grad_values + jnp.einsum('hqk,qhd->khd', probs_b.astype(jnp.float32), part_g.astype(jnp.float32))
        grad_probs = jnp.einsum('qhd,khd->hqk', part_g.astype(jnp.float32), values.astype(jnp.float32))
        delta = lax.optimization_barrier(jnp.sum(probs * grad_probs, -1, keepdims=True))
        grad_scores = (probs * (grad_probs - delta) * scale).astype(jnp.bfloat16)
        grad_part = jnp.einsum('hqk,khd->qhd', grad_scores.astype(jnp.float32), keys_b.astype(jnp.float32))
        grad_keys = grad_keys + jnp.einsum('hqk,qhd->khd', grad_scores.astype(jnp.float32), part_q.astype(jnp.float32))
        return ((grad_keys, grad_values), grad_part)
    zeros_kv = jnp.zeros((length, heads_here, head_dim), jnp.float32)
    (grad_keys, grad_values), grad_queries = lax.scan(one_block, (zeros_kv, zeros_kv), jnp.arange(count, dtype=jnp.int32))
    return (grad_queries.reshape(length, heads_here, head_dim), grad_keys, grad_values)

def normal_cdf(values):
    return 0.5 * (1.0 + lax.erf(values * (1.0 / math.sqrt(2.0))))

def gelu_slope(values):
    return normal_cdf(values) + values * jnp.exp(-0.5 * values * values) * (1.0 / math.sqrt(2.0 * math.pi))

def one_pack(block_in, cotangent, segments, positions, attn_gain, attn_shift, mlp_gain, mlp_shift, qkv_weight, qkv_bias, out_weight, out_bias, up_weight, up_bias, down_weight, down_bias):
    length = block_in.shape[0]
    residual = block_in.astype(jnp.float32)
    average = lax.optimization_barrier(jnp.mean(residual, -1, keepdims=True))
    spread = lax.optimization_barrier(jnp.mean(residual * residual, -1, keepdims=True)) - average * average
    inv_std = lax.rsqrt(spread + EPS)
    normal = (residual - average) * inv_std
    attn_in = (normal * attn_gain + attn_shift).astype(jnp.bfloat16)
    mlp_in = (normal * mlp_gain + mlp_shift).astype(jnp.bfloat16)
    merged = jnp.dot(attn_in, qkv_weight, preferred_element_type=jnp.float32) + qkv_bias
    packed = merged.reshape(length, HEADS, 3, HD)
    cosine, sine_tab = rotary_tables(positions, ROT)
    queries = rotate_fwd(packed[:, :, 0], cosine, sine_tab).astype(jnp.bfloat16)
    keys_b = rotate_fwd(packed[:, :, 1], cosine, sine_tab).astype(jnp.bfloat16)
    values = packed[:, :, 2].astype(jnp.bfloat16)
    attended, log_total = attend(queries, keys_b, values, segments)
    attended = attended.reshape(length, D).astype(jnp.bfloat16)
    up_proj = jnp.dot(mlp_in, up_weight, preferred_element_type=jnp.float32) + up_bias
    activated = (up_proj * normal_cdf(up_proj)).astype(jnp.bfloat16)
    mixed = jnp.dot(attended, out_weight, preferred_element_type=jnp.float32) + jnp.dot(activated, down_weight, preferred_element_type=jnp.float32)
    block_out = (mixed + out_bias + down_bias + residual).astype(jnp.bfloat16)
    grad_y = cotangent.astype(jnp.float32)
    grad_bias_out = lax.optimization_barrier(jnp.sum(grad_y, 0))
    grad_out_w = jnp.dot(attended.T, cotangent, preferred_element_type=jnp.float32)
    grad_down_w = jnp.dot(activated.T, cotangent, preferred_element_type=jnp.float32)
    grad_att = jnp.dot(cotangent, out_weight.T, preferred_element_type=jnp.float32).astype(jnp.bfloat16).reshape(length, HEADS, HD)
    grad_act = jnp.dot(cotangent, down_weight.T, preferred_element_type=jnp.float32)
    grad_up = grad_act * gelu_slope(up_proj)
    grad_queries, grad_keys, grad_values = attend_back(queries, keys_b, values, grad_att, log_total, segments)
    grad_queries = rotate_back(grad_queries, cosine, sine_tab)
    grad_keys = rotate_back(grad_keys, cosine, sine_tab)
    grad_merged = jnp.stack([grad_queries, grad_keys, grad_values], 2).reshape(length, 3 * D)
    grad_qkv_b = lax.optimization_barrier(jnp.sum(grad_merged, 0))
    grad_up_b = lax.optimization_barrier(jnp.sum(grad_up, 0))
    merged_b = grad_merged.astype(jnp.bfloat16)
    up_b = grad_up.astype(jnp.bfloat16)
    grad_qkv_w = jnp.dot(attn_in.T, merged_b, preferred_element_type=jnp.float32)
    grad_up_w = jnp.dot(mlp_in.T, up_b, preferred_element_type=jnp.float32)
    grad_attn_in = jnp.dot(merged_b, qkv_weight.T, preferred_element_type=jnp.float32)
    grad_mlp_in = jnp.dot(up_b, up_weight.T, preferred_element_type=jnp.float32)
    grad_ag = lax.optimization_barrier(jnp.sum(grad_attn_in * normal, 0))
    grad_as = lax.optimization_barrier(jnp.sum(grad_attn_in, 0))
    grad_mg = lax.optimization_barrier(jnp.sum(grad_mlp_in * normal, 0))
    grad_ms = lax.optimization_barrier(jnp.sum(grad_mlp_in, 0))
    grad_normal = grad_attn_in * attn_gain + grad_mlp_in * mlp_gain
    grad_x = grad_y + inv_std * (grad_normal - lax.optimization_barrier(jnp.mean(grad_normal, -1, keepdims=True)) - normal * lax.optimization_barrier(jnp.mean(grad_normal * normal, -1, keepdims=True)))
    grads = (grad_qkv_w, grad_qkv_b, grad_out_w, grad_bias_out, grad_up_w, grad_up_b, grad_down_w, grad_ag, grad_as, grad_mg, grad_ms)
    return (block_out, grad_x.astype(jnp.bfloat16), grads)

def reference(block_in, cotangent, segments, positions, attn_gain, attn_shift, mlp_gain, mlp_shift, qkv_weight, qkv_bias, out_weight, out_bias, up_weight, up_bias, down_weight, down_bias):
    packs_in = block_in.reshape(N_DP, PACK, D)
    packs_cot = cotangent.reshape(N_DP, PACK, D)
    packs_seg = segments.reshape(N_DP, PACK)
    packs_pos = positions.reshape(N_DP, PACK)
    start = (jnp.zeros((D, 3 * D), jnp.float32), jnp.zeros((3 * D,), jnp.float32), jnp.zeros((D, D), jnp.float32), jnp.zeros((D,), jnp.float32), jnp.zeros((D, FF), jnp.float32), jnp.zeros((FF,), jnp.float32), jnp.zeros((FF, D), jnp.float32), jnp.zeros((D,), jnp.float32), jnp.zeros((D,), jnp.float32), jnp.zeros((D,), jnp.float32), jnp.zeros((D,), jnp.float32))

    def step_pack(carry, items):
        part_in, part_cot, part_seg, part_pos = items
        block_out, grad_x, grads = one_pack(part_in, part_cot, part_seg, part_pos, attn_gain, attn_shift, mlp_gain, mlp_shift, qkv_weight, qkv_bias, out_weight, out_bias, up_weight, up_bias, down_weight, down_bias)
        carry = tuple((total + piece for total, piece in zip(carry, grads)))
        return (carry, (block_out, grad_x))
    totals, (outs, grads_x) = lax.scan(step_pack, start, (packs_in, packs_cot, packs_seg, packs_pos))
    return (outs.reshape(TOKENS, D), grads_x.reshape(TOKENS, D), totals[0], totals[1], totals[2], totals[3], totals[4], totals[5], totals[6], totals[3], totals[7], totals[8], totals[9], totals[10])
```

```python
import math

import jax
import jax.numpy as jnp
from jax import lax
from jax.experimental import pallas as pl
from jax.experimental.pallas import tpu as pltpu
from jax.sharding import PartitionSpec as P

D = 1024
HD = 64
ROT = 16
EPS = 1e-05
NEG = -1e30
BF = jnp.bfloat16
F32 = jnp.float32


def swap(value, axis, mask):
    size = lax.axis_size(axis)
    return lax.ppermute(value, axis, [(i, i ^ mask) for i in range(size)])


def bit_reversed(count):
    bits = count.bit_length() - 1
    return [int(format(i, "b").zfill(bits)[::-1], 2) if bits else 0 for i in range(count)]


def dot(a, b):
    return jnp.dot(a, b, preferred_element_type=F32)


def dot_nt(a, b):
    return lax.dot_general(a, b, (((1,), (1,)), ((), ())), preferred_element_type=F32)


def dot_tn(a, b):
    return lax.dot_general(a, b, (((0,), (0,)), ((), ())), preferred_element_type=F32)


def normal_cdf(values):
    return 0.5 * (1.0 + lax.erf(values * (1.0 / math.sqrt(2.0))))


def place(pieces, where, parts, row_map, rows_out, cols_out):
    split = sum(p.shape[0] for p in pieces)
    order = bit_reversed(split)
    cols = pieces[0].shape[1]

    def body(where_ref, *refs):
        ins = refs[: len(pieces)]
        outs = refs[len(pieces) :]
        share = where_ref[0]
        col = where_ref[1]
        at = 0
        for ref in ins:
            for local in range(ref.shape[0]):
                natural = share ^ order[at]
                for k in range(cols):
                    from_col = col ^ k
                    for out_ref, (low, rows, by_rows) in zip(outs, parts):
                        value = ref[local, k, low : low + rows, :].astype(F32)
                        width = value.shape[1]
                        if by_rows:
                            start = pl.multiple_of(from_col * (rows * split) + natural * rows, rows)
                            out_ref[pl.ds(start, rows), :] = value
                        else:
                            top = pl.multiple_of(natural * rows, rows)
                            left = pl.multiple_of(from_col * width, 128)
                            out_ref[pl.ds(top, rows), pl.ds(left, width)] = value
                at += 1

    return pl.pallas_call(
        body,
        out_shape=[jax.ShapeDtypeStruct((r, w), F32) for r, w in zip(rows_out, cols_out)],
        in_specs=[pl.BlockSpec(memory_space=pltpu.SMEM)]
        + [pl.BlockSpec(memory_space=pltpu.VMEM)] * len(pieces),
        out_specs=[pl.BlockSpec(memory_space=pltpu.VMEM)] * len(parts),
        name=row_map,
    )(where, *pieces)


def shards(
    block_in,
    cotangent,
    segments,
    positions,
    attn_gain,
    attn_shift,
    mlp_gain,
    mlp_shift,
    qkv_weight,
    qkv_bias,
    out_weight,
    out_bias,
    up_weight,
    up_bias,
    down_weight,
    down_bias,
):
    n_dp = lax.axis_size("dp")
    n_col = lax.axis_size("col")
    n_row = lax.axis_size("row")
    split = min(4, n_dp)
    bits = split.bit_length() - 1
    order = bit_reversed(split)
    share = lax.axis_index("dp") % split
    col = lax.axis_index("col")
    row = lax.axis_index("row")
    half, width = block_in.shape
    length = segments.shape[0]
    qkv_share = qkv_weight.shape[1] // n_col
    up_share = up_weight.shape[1] // n_col
    heads = qkv_share // (3 * HD)
    att = heads * HD
    sub = width // split
    out_sub = att // split
    down_sub = up_share // split
    where = jnp.stack([share, col, row]).astype(jnp.int32)

    def col_all(value):
        return [value] + [swap(value, "col", k) for k in range(1, n_col)]

    def grid_gather(value):
        mine = col_all(value)
        other = [swap(v, "row", 1) for v in mine]
        return jnp.concatenate([jnp.concatenate(mine, 1), jnp.concatenate(other, 1)], 0)

    def share_gather(value):
        for bit in reversed(range(bits)):
            value = jnp.concatenate([value, swap(value, "dp", 1 << bit)], 0)
        return value

    def natural(value, axis):
        pieces = [
            lax.dynamic_index_in_dim(value, 0, 0, keepdims=True) for _ in range(0)
        ]
        table = jnp.array(order, jnp.int32)
        for j in range(split):
            at = table[share ^ j]
            pieces.append(lax.dynamic_index_in_dim(value, at, 0, keepdims=False))
        return jnp.stack(pieces, axis)

    gains = jnp.stack([attn_gain, attn_shift, mlp_gain, mlp_shift])
    x = grid_gather(block_in)
    gains_k = col_all(gains)
    gains = jnp.concatenate(gains_k, 1)

    first = []
    for k in range(n_col):
        q_part = lax.dynamic_slice(
            qkv_weight, (share * sub, (col ^ k) * qkv_share), (sub, qkv_share)
        )
        q_part = q_part.reshape(sub, heads, 3, HD).transpose(0, 2, 1, 3).reshape(sub, qkv_share)
        u_part = lax.dynamic_slice(
            up_weight, (share * sub, (col ^ k) * up_share), (sub, up_share)
        )
        piece = jnp.concatenate([q_part, u_part], 1)
        first.append(swap(piece, "col", k) if k else piece)
    first = share_gather(jnp.stack(first)[None])
    first = natural(first, 1).reshape(n_col * width, qkv_share + up_share)
    w_qkv = first[:, :qkv_share]
    w_up = first[:, qkv_share:]

    cot = grid_gather(cotangent)
    second = []
    for k in range(n_col):
        o_part = lax.dynamic_slice(
            out_weight, ((col ^ k) * att + share * out_sub, 0), (out_sub, width)
        )
        d_part = lax.dynamic_slice(
            down_weight, ((col ^ k) * up_share + share * down_sub, 0), (down_sub, width)
        )
        piece = jnp.concatenate([o_part, d_part], 0)
        second.append(swap(piece, "col", k) if k else piece)
    second = share_gather(jnp.stack(second)[None])
    second = natural(second, 0)
    second = second.transpose(0, 2, 1, 3).reshape(split, out_sub + down_sub, n_col * width)
    w_out = second[:, :out_sub].reshape(att, n_col * width)
    w_down = second[:, out_sub:].reshape(up_share, n_col * width)

    def own_first(v):
        return jnp.where(row == 0, v, jnp.concatenate([v[half:], v[:half]]))

    pos = own_first(positions)
    seg = own_first(segments)
    tok = own_first(jnp.arange(length, dtype=jnp.int32))
    half_dims = ROT // 2
    inverse = jnp.power(10000.0, -jnp.arange(half_dims, dtype=F32) * (2.0 / ROT))
    angles = pos.astype(F32)[:, None] * inverse[None, :]
    cosine = jnp.cos(angles)
    sine = jnp.sin(angles)
    rest = HD - ROT
    zero8 = jnp.zeros_like(sine)
    cos_t = jnp.tile(
        jnp.concatenate([cosine, cosine, jnp.ones((length, rest), F32)], 1), (1, heads)
    )
    sin_a = jnp.tile(
        jnp.concatenate([-sine, zero8, jnp.zeros((length, rest), F32)], 1), (1, heads)
    )
    sin_b = jnp.tile(
        jnp.concatenate([zero8, sine, jnp.zeros((length, rest), F32)], 1), (1, heads)
    )

    def turn(u, sign):
        return (
            u * cos_t
            + jnp.roll(u, -half_dims, 1) * (sign * sin_a)
            + jnp.roll(u, half_dims, 1) * (sign * sin_b)
        )

    allowed = (tok[None, :] <= tok[:, None]) & (seg[None, :] == seg[:, None])

    residual = x.astype(F32)
    average = jnp.sum(residual, 1, keepdims=True) / D
    spread = jnp.sum(residual * residual, 1, keepdims=True) / D - average * average
    inv_std = lax.rsqrt(spread + EPS)
    normal = (residual - average) * inv_std
    attn_in = (normal * gains[0] + gains[1]).astype(BF)
    mlp_in = (normal * gains[2] + gains[3]).astype(BF)
    b_qkv = qkv_bias.reshape(heads, 3, HD).transpose(1, 0, 2).reshape(qkv_share)
    merged = dot(attn_in, w_qkv) + b_qkv
    up_proj = dot(mlp_in, w_up) + up_bias
    queries = turn(merged[:, :att], 1.0).astype(BF)
    keys_b = turn(merged[:, att : 2 * att], 1.0).astype(BF)
    values = merged[:, 2 * att :].astype(BF)
    cdf = normal_cdf(up_proj)
    activated = (up_proj * cdf).astype(BF)
    slope = cdf + up_proj * jnp.exp(-0.5 * up_proj * up_proj) * (1.0 / math.sqrt(2.0 * math.pi))

    attended = []
    probs_h = []
    for h in range(heads):
        lanes = slice(h * HD, (h + 1) * HD)
        scores = dot_nt(queries[:, lanes], keys_b[:, lanes]) * (1.0 / math.sqrt(HD))
        scores = jnp.where(allowed, scores, NEG)
        top = jnp.max(scores, -1, keepdims=True)
        expo = jnp.exp(scores - top)
        probs = expo / jnp.sum(expo, -1, keepdims=True)
        probs_h.append(probs)
        attended.append(dot(probs.astype(BF), values[:, lanes]))
    attended = jnp.concatenate(attended, 1).astype(BF)

    def grid_scatter(value):
        value = value.astype(BF)
        got = swap(value[half:], "row", 1)
        both = (value[:half].astype(F32) + got.astype(F32)).astype(BF)
        total = both[:, :width].astype(F32)
        for k in range(1, n_col):
            total = total + swap(both[:, k * width : (k + 1) * width], "col", k).astype(F32)
        return total

    mixed = grid_scatter(dot(attended, w_out) + dot(activated, w_down))
    block_out = (mixed + out_bias + down_bias + block_in.astype(F32)).astype(BF)

    def share_reduce(value):
        for bit in range(bits):
            keep = value.shape[0] // 2
            got = swap(value[keep:], "dp", 1 << bit)
            value = (value[:keep].astype(F32) + got.astype(F32)).astype(BF)
        step = split
        while step < n_dp:
            value = (value.astype(F32) + swap(value, "dp", step).astype(F32)).astype(BF)
            step *= 2
        return value[0]

    def own_order(value):
        table = jnp.array(order, jnp.int32)
        pieces = []
        for p in range(split):
            pieces.append(lax.dynamic_index_in_dim(value, share ^ table[p], 0, keepdims=False))
        return jnp.stack(pieces)

    def weight_grad(value, parts, rows_out, cols_out, name):
        value = share_reduce(own_order(value.astype(BF)))
        moved = [value[:1]] + [swap(value[k : k + 1], "col", k) for k in range(1, n_col)]
        value = share_gather(jnp.concatenate(moved, 0)[None])
        return place([value], where, parts, name, rows_out, cols_out)

    grad_down = dot_tn(activated, cot).reshape(split, down_sub, n_col, width).transpose(0, 2, 1, 3)
    grad_out = dot_tn(attended, cot).reshape(split, out_sub, n_col, width).transpose(0, 2, 1, 3)
    out_g, down_g = weight_grad(
        jnp.concatenate([grad_out, grad_down], 2),
        [(0, out_sub, True), (out_sub, down_sub, True)],
        [att * n_col, up_share * n_col],
        [width, width],
        "place_out",
    )
    grad_act = dot_nt(cot, w_down)
    grad_att = dot_nt(cot, w_out).astype(BF)
    grad_up = grad_act * slope
    grad_up_bias = jnp.sum(grad_up, 0)
    grad_up_b = grad_up.astype(BF)
    grad_up_w = dot_tn(mlp_in, grad_up_b).reshape(n_col, split, sub, up_share).transpose(1, 0, 2, 3)
    (up_g,) = weight_grad(
        grad_up_w, [(0, sub, False)], [width], [up_share * n_col], "place_up"
    )
    grad_mlp_in = dot_nt(grad_up_b, w_up)

    grad_q = []
    grad_k = []
    grad_v = []
    for h in range(heads):
        lanes = slice(h * HD, (h + 1) * HD)
        probs = probs_h[h]
        g_att = grad_att[:, lanes]
        grad_v.append(dot_tn(probs.astype(BF), g_att))
        grad_probs = dot_nt(g_att, values[:, lanes])
        delta = jnp.sum(probs * grad_probs, -1, keepdims=True)
        grad_scores = (probs * (grad_probs - delta) * (1.0 / math.sqrt(HD))).astype(BF)
        grad_q.append(dot(grad_scores, keys_b[:, lanes]))
        grad_k.append(dot_tn(grad_scores, queries[:, lanes]))
    grad_q = turn(jnp.concatenate(grad_q, 1), -1.0)
    grad_k = turn(jnp.concatenate(grad_k, 1), -1.0)
    grad_v = jnp.concatenate(grad_v, 1)
    grad_merged = jnp.concatenate([grad_q, grad_k, grad_v], 1)
    grad_qkv_bias = jnp.sum(grad_merged, 0)
    grad_merged = grad_merged.astype(BF)
    grad_attn_in = dot_nt(grad_merged, w_qkv)
    grad_normal_part = grad_attn_in * gains[0] + grad_mlp_in * gains[2]
    sums = jnp.stack(
        [jnp.sum(grad_normal_part, 1), jnp.sum(grad_normal_part * normal, 1)]
    )
    norm_sums = jnp.stack(
        [
            jnp.sum(grad_attn_in * normal, 0),
            jnp.sum(grad_attn_in, 0),
            jnp.sum(grad_mlp_in * normal, 0),
            jnp.sum(grad_mlp_in, 0),
        ]
    )
    grad_normal = grid_scatter(grad_normal_part)
    sums = sums[:, :half] + swap(sums[:, half:], "row", 1)
    step = 1
    while step < n_col:
        sums = sums + swap(sums, "col", step)
        step *= 2
    own_normal = normal[:half, :width]
    grad_x = cotangent.astype(F32) + inv_std[:half] * (
        grad_normal - sums[0][:, None] / D - own_normal * (sums[1][:, None] / D)
    )

    grad_qkv_w = dot_tn(attn_in, grad_merged)
    grad_qkv_w = (
        grad_qkv_w.reshape(-1, 3, heads, HD).transpose(0, 2, 1, 3).reshape(-1, qkv_share)
    )
    grad_qkv_w = grad_qkv_w.reshape(n_col, split, sub, qkv_share).transpose(1, 0, 2, 3)
    (qkv_g,) = weight_grad(
        grad_qkv_w, [(0, sub, False)], [width], [qkv_share * n_col], "place_qkv"
    )

    norm_sums = norm_sums + swap(norm_sums, "row", 1)
    total = norm_sums[:, :width]
    for k in range(1, n_col):
        total = total + swap(norm_sums[:, k * width : (k + 1) * width], "col", k)
    grad_bias = jnp.sum(cot[:, :width].astype(F32), 0)
    smalls = jnp.concatenate([total.reshape(-1), grad_qkv_bias, grad_up_bias, grad_bias])
    step = 1
    while step < n_dp:
        smalls = smalls + swap(smalls, "dp", step)
        step *= 2
    norm = smalls[: 4 * width].reshape(4, width)
    at = 4 * width
    qkv_b = smalls[at : at + qkv_share].reshape(3, heads, HD).transpose(1, 0, 2).reshape(-1)
    at += qkv_share
    up_b = smalls[at : at + up_share]
    at += up_share
    bias_g = smalls[at:]
    return (
        block_out,
        grad_x.astype(BF),
        qkv_g,
        qkv_b,
        out_g,
        bias_g,
        up_g,
        up_b,
        down_g,
        bias_g,
        norm[0],
        norm[1],
        norm[2],
        norm[3],
    )


def solution(mesh):
    return jax.shard_map(
        shards,
        mesh=mesh,
        in_specs=(
            P(("dp", "row"), "col"),
            P(("dp", "row"), "col"),
            P("dp"),
            P("dp"),
            P("col"),
            P("col"),
            P("col"),
            P("col"),
            P("col", "row"),
            P(("row", "col")),
            P("row", "col"),
            P("col"),
            P("col", "row"),
            P(("row", "col")),
            P("row", "col"),
            P("col"),
        ),
        out_specs=(
            P(("dp", "row"), "col"),
            P(("dp", "row"), "col"),
            P("col", "row"),
            P(("row", "col")),
            P("row", "col"),
            P("col"),
            P("col", "row"),
            P(("row", "col")),
            P("row", "col"),
            P("col"),
            P("col"),
            P("col"),
            P("col"),
            P("col"),
        ),
        check_vma=False,
    )
```
